32 devices in a mesh: dp: 8 (over z, x), owner: 4 (over y, core).
Axes of the slice: x: 2, y: 2, z: 4, core: 2. Of those that a mesh axis runs over, the one named last changes fastest.
Arguments:
- layer_input: bfloat16 [2048, 8192], P('dp', 'owner'), may hold values from -6 to 6
- output_grads: bfloat16 [2048, 10240], P('dp', 'owner'), may hold values from -6 to 6
- projection: bfloat16 [8192, 10240], P('owner', 'dp'), may hold values from -0.0625 to 0.0625
Outputs:
- grad_input: bfloat16 [2048, 8192], P('dp', 'owner')
- update_query: bfloat16 [8192, 8192], P('owner', 'dp')
- update_kv: bfloat16 [8192, 2048], P('owner', 'dp')
The draws below stay inside these ranges and needn't reach their ends.
All inputs are finite; a program needn't handle non-finite values.
Results may differ from the reference program's by a relative error of at most 0.023.
Values may be sent and summed in bfloat16 or wider, within the bound.
No kernel may reach another device: no remote copies, remote signals or barrier semaphores. Data moves between devices by JAX's collectives and lax.ppermute only.
A program may use at most 192 MiB of HBM per device.

```python
import math
import jax
import jax.numpy as jnp
from jax import lax

D = 8192
BLOCK = 512
TOK_DEV = 256
QW = 8192
KVW = 2048
COLS = 10240
TOKENS = 2048
N_DP = 8


def strengthened(drawn, own_key, source, target, parts, factor):
    owner, partner = [(jnp.arange(drawn.shape[axis_at]) // (drawn.shape[axis_at] // parts)).reshape([-1 if axis == axis_at else 1 for axis in range(drawn.ndim)]) for axis_at in (source, target)]
    chosen = jax.random.permutation(own_key, parts)[partner]
    strong = (owner == chosen) | (owner == (partner + parts // 2) % parts)
    return jnp.where(strong, factor * drawn, drawn)


def steps_of(own_key, dims, cuts, low, largest):
    def one(axis_at, shards_of):
        heights = jax.random.uniform(jax.random.fold_in(jax.random.fold_in(own_key, 6), axis_at), (shards_of,), jnp.float32, low / len(cuts), largest / len(cuts))
        return jnp.repeat(jnp.exp(heights), dims[axis_at] // shards_of).reshape((-1,) + (1,) * (len(dims) - axis_at - 1))

    gain = one(*cuts[0])
    for cut in cuts[1:]:
        gain = gain * one(*cut)
    return gain


def gaussian(stream_key, dims, spread, reach, cuts=(), kind=jnp.bfloat16):
    array = jax.random.normal(stream_key, dims, jnp.float32) * spread
    if len(cuts) > 0:
        array = steps_of(stream_key, dims, cuts, -0.22, 0.18) * array
    return jnp.clip(array, min=-reach, max=reach).astype(kind)


def heavy_noise(stream_key, extent, spread, bound, cuts, heavy, kind=jnp.bfloat16):
    entries = spread * jax.random.normal(stream_key, extent, jnp.float32)
    if cuts:
        entries = entries * steps_of(stream_key, extent, cuts, -0.22, 0.18)
    return jnp.clip(strengthened(entries, jax.random.fold_in(stream_key, 3), *heavy), -bound, bound).astype(kind)


def setup_inputs(seed: int = 0) -> dict:
    keys = jax.random.split(jax.random.key(seed), 4)
    layer_input = gaussian(keys[0], (TOKENS, D), 1.0, 6.0, ((0, 8), (1, 4)))
    output_grads = heavy_noise(keys[1], (TOKENS, COLS), 1.0, 6.0, ((0, 8), (1, 4)), (0, 1, 8, 2.0))
    projection = gaussian(keys[2], (D, COLS), D ** -0.5, 0.0625, ((0, 4), (1, 8)))
    return {"layer_input": layer_input, "output_grads": output_grads, "projection": projection}


def left_stat(blocks):
    floats = blocks.astype(jnp.float32)
    return jnp.einsum('...ij,...kj->...ik', floats, floats, precision=lax.Precision.HIGHEST)

def right_stat(blocks):
    floats = blocks.astype(jnp.float32)
    return jnp.einsum('...ji,...jk->...ik', floats, floats, precision=lax.Precision.HIGHEST)

def inverse_root(statistic):
    width = statistic.shape[-1]
    scale = math.sqrt(width) * jnp.sqrt(lax.optimization_barrier(jnp.mean(statistic * statistic, axis=(-2, -1), keepdims=True)) + 1e-06)
    normed = statistic / scale
    identity = jnp.eye(width, dtype=jnp.float32)
    return scale ** (-0.25) * (5.0 * identity - normed) * 0.25

def precondition(blocks):
    width = blocks.shape[-1]
    root_left = inverse_root(left_stat(blocks))
    root_right = inverse_root(right_stat(blocks))
    half = jnp.einsum('...ij,...jk->...ik', blocks.astype(jnp.float32), root_right, precision=lax.Precision.HIGHEST)
    whole = jnp.einsum('...ij,...jk->...ik', root_left, half, precision=lax.Precision.HIGHEST)
    return (whole * math.sqrt(width)).astype(jnp.bfloat16)

def update_rows(rowset):
    columns = rowset.shape[1]
    blocks = rowset.reshape(BLOCK, columns // BLOCK, BLOCK).transpose(1, 0, 2)
    return precondition(blocks).transpose(1, 0, 2).reshape(BLOCK, columns)

def reference(layer_input, output_grads, projection):
    grad_input = jnp.dot(output_grads, projection.T, preferred_element_type=jnp.float32).astype(jnp.bfloat16)
    inputs_grouped = layer_input.reshape(N_DP, TOK_DEV, layer_input.shape[1])
    grads_grouped = output_grads.reshape(N_DP, TOK_DEV, output_grads.shape[1])

    def accumulate(running, pair):
        partial_value = jnp.dot(pair[0].T, pair[1], preferred_element_type=jnp.float32).astype(jnp.bfloat16)
        partial_value = lax.optimization_barrier(partial_value)
        return (running + partial_value.astype(jnp.float32), None)
    initial = jnp.zeros((layer_input.shape[1], output_grads.shape[1]), jnp.float32)
    summed, _ = lax.scan(accumulate, initial, (inputs_grouped, grads_grouped))
    gradient = summed.astype(jnp.bfloat16)
    rowsets = gradient.reshape(gradient.shape[0] // BLOCK, BLOCK, gradient.shape[1])
    update_query = lax.map(update_rows, rowsets[:, :, :QW]).reshape(gradient.shape[0], QW)
    update_kv = lax.map(update_rows, rowsets[:, :, QW:]).reshape(gradient.shape[0], KVW)
    return (grad_input, update_query, update_kv)
```

```python
import functools
import math

import jax
import jax.numpy as jnp
import numpy as np
from jax import lax
from jax.experimental import pallas as pl
from jax.experimental.pallas import tpu as pltpu
from jax.sharding import PartitionSpec as P

BLOCK = 512
QW = 8192


def inner_size(n):
    return 1 << (int(math.log2(n)) // 2)


def swap_owner(x, mask, n_owner):
    return lax.ppermute(x, "owner", [(i, i ^ mask) for i in range(n_owner)])


def spread_owner(x, n_owner):
    pieces = {0: x}
    bit = n_owner // 2
    while bit:
        pieces.update({k | bit: swap_owner(p, bit, n_owner) for k, p in pieces.items()})
        bit //= 2
    return [pieces[k] for k in range(n_owner)]


def pair_kernel(tab, *refs, n_owner, pair):
    xs, w_ref, o_ref = refs[: pair * n_owner], refs[-2], refs[-1]
    rows = jnp.concatenate([r[0] for r in xs], axis=0)
    out = lax.dot_general(
        rows, w_ref[...], (((1,), (1,)), ((), ())), preferred_element_type=jnp.float32
    )
    o_ref[...] = out.astype(o_ref.dtype).reshape(o_ref.shape)


def pair_product(tab, pieces, w, tile=512):
    n_owner, pair = len(pieces), tab.shape[0]
    _, tq, cols = pieces[0].shape
    feats = w.shape[0]
    tile = min(tile, feats)
    xspec = [
        pl.BlockSpec((1, tq, cols), lambda j, t, i=i: (t[i], 0, 0))
        for i in range(pair)
        for _ in range(n_owner)
    ]
    return pl.pallas_call(
        functools.partial(pair_kernel, n_owner=n_owner, pair=pair),
        grid_spec=pltpu.PrefetchScalarGridSpec(
            num_scalar_prefetch=1,
            grid=(feats // tile,),
            in_specs=xspec + [pl.BlockSpec((tile, cols), lambda j, t: (j, 0))],
            out_specs=pl.BlockSpec((pair, n_owner * tq, tile), lambda j, t: (0, 0, j)),
        ),
        out_shape=jax.ShapeDtypeStruct((pair, n_owner * tq, feats), jnp.bfloat16),
        compiler_params=pltpu.CompilerParams(vmem_limit_bytes=40 << 20),
        cost_estimate=pl.CostEstimate(
            flops=2 * pair * n_owner * tq * cols * feats,
            bytes_accessed=2 * (feats * cols + pair * n_owner * tq * (cols + feats)),
            transcendentals=0,
        ),
        name="pair_product",
    )(tab, *(pieces * pair), w)


def update_kernel(tab, l_ref, *refs, n_owner):
    xs, o_ref = refs[:n_owner], refs[-1]
    width = o_ref.shape[-1]
    acc = None
    for k in range(n_owner):
        left = l_ref[:, tab[0] ^ k]
        left = left.reshape(-1, width)
        right = xs[k][...].reshape(-1, width)
        term = lax.dot_general(
            left, right, (((0,), (0,)), ((), ())), preferred_element_type=jnp.float32
        )
        acc = term if acc is None else acc + term
    g = acc.astype(jnp.bfloat16)
    stat = lax.dot_general(
        g, g, (((1,), (1,)), ((), ())), preferred_element_type=jnp.float32
    )
    mean = jnp.sum(stat * stat) * (1.0 / (width * width))
    scale = math.sqrt(width) * jnp.sqrt(jnp.full((1, 1), mean + 1e-06))
    normed = (stat * (1.0 / scale)).astype(jnp.bfloat16)
    once = 5.0 * g.astype(jnp.float32) - jnp.dot(
        normed, g, preferred_element_type=jnp.float32
    )
    twice = 5.0 * once - jnp.dot(
        normed, once.astype(jnp.bfloat16), preferred_element_type=jnp.float32
    )
    factor = (math.sqrt(width) / 16.0) * lax.rsqrt(scale)
    o_ref[...] = (twice * factor).astype(o_ref.dtype)


def block_updates(tab, inputs, pieces, first_col, n_rows, n_cols):
    count, n_owner, tq, _ = inputs.shape
    width = BLOCK
    tokens = count * n_owner * tq
    return pl.pallas_call(
        functools.partial(update_kernel, n_owner=n_owner),
        grid_spec=pltpu.PrefetchScalarGridSpec(
            num_scalar_prefetch=1,
            grid=(n_rows, n_cols),
            in_specs=[
                pl.BlockSpec((count, n_owner, tq, width), lambda r, c, t: (0, 0, 0, r + t[1]))
            ]
            + [
                pl.BlockSpec((count, tq, width), lambda r, c, t: (0, 0, c + first_col))
                for _ in range(n_owner)
            ],
            out_specs=pl.BlockSpec((width, width), lambda r, c, t: (r, c)),
        ),
        out_shape=jax.ShapeDtypeStruct((n_rows * width, n_cols * width), jnp.bfloat16),
        compiler_params=pltpu.CompilerParams(vmem_limit_bytes=56 << 20),
        cost_estimate=pl.CostEstimate(
            flops=n_rows * n_cols * (2 * tokens * width * width + 6 * width**3),
            bytes_accessed=2 * n_rows * n_cols * tokens * width * 2,
            transcendentals=0,
        ),
        name="block_updates",
    )(tab, inputs, *pieces)


def scatter_sum(products, n_dp, z, x, outer, inner):
    order = np.zeros((outer, outer), np.int32)
    for i in range(outer):
        order[i] = sorted(range(outer), key=lambda t: (-abs(t - i), t != i and t < i))
    slot = np.argsort(order, axis=1)
    order_c = jnp.asarray(order)
    sums = []
    for k in range(outer):
        target = order_c[z, k]
        groups = jnp.stack([target * inner + (x + s) % inner for s in range(inner)])
        part = products(groups)
        total = part[0].astype(jnp.float32)
        for s in range(1, inner):
            pairs = [
                (a * inner + b, a * inner + (b + s) % inner)
                for a in range(outer)
                for b in range(inner)
            ]
            total = total + lax.ppermute(part[s], "dp", pairs).astype(jnp.float32)
        sums.append(total.astype(jnp.bfloat16))

    def chosen(step, sign):
        table = np.zeros(outer, np.int32)
        pairs = []
        for i in range(outer):
            target = i + sign * (outer - step)
            if 0 <= target < outer:
                table[i] = slot[i, target]
                pairs += [
                    (i * inner + b, (i + sign) * inner + b) for b in range(inner)
                ]
        used = sorted(set(table[[p[0] // inner for p in pairs]].tolist()))
        value = sums[used[0]]
        for u in used[1:]:
            value = jnp.where(jnp.asarray(table)[z] == u, sums[u], value)
        return value, pairs

    running = {1: None, -1: None}
    for step in range(1, outer):
        for sign in (1, -1):
            value, pairs = chosen(step, sign)
            if running[sign] is not None:
                value = (value.astype(jnp.float32) + running[sign].astype(jnp.float32)).astype(
                    jnp.bfloat16
                )
            running[sign] = lax.ppermute(value, "dp", pairs)
    own = sums[outer - 1].astype(jnp.float32)
    if outer > 1:
        own = own + running[1].astype(jnp.float32) + running[-1].astype(jnp.float32)
    return own.astype(jnp.bfloat16)


def body(layer_input, output_grads, projection):
    n_dp, n_owner = lax.axis_size("dp"), lax.axis_size("owner")
    dp, owner = lax.axis_index("dp"), lax.axis_index("owner")
    inner = inner_size(n_dp)
    outer = n_dp // inner
    z, x = dp // inner, dp % inner
    group, rows_own = layer_input.shape
    cols_own = projection.shape[1]
    all_cols = cols_own * n_dp
    tq = group // n_owner
    q_own = QW // n_dp
    kv_own = (all_cols - QW) // n_dp
    sharers = max(1, BLOCK // kv_own)
    kv_need = max(kv_own, BLOCK)
    row_blocks = rows_own // BLOCK

    gathered = lax.all_gather(layer_input, "dp", axis=0, tiled=True)
    inputs = gathered.reshape(n_dp, n_owner, tq, rows_own)

    spread = lax.all_to_all(
        output_grads.reshape(n_owner, tq, output_grads.shape[1]), "owner", 0, 0
    )
    flat = jnp.transpose(spread, (1, 0, 2)).reshape(tq, all_cols)
    first = jnp.transpose(flat.reshape(tq, n_dp, cols_own), (1, 0, 2))
    first = lax.all_to_all(first, "dp", 0, 0)
    first = spread_owner(first, n_owner)
    query = flat[:, :QW].reshape(tq, n_dp, q_own)
    kv = flat[:, QW:].reshape(tq, n_dp // sharers, 1, kv_need)
    kv = jnp.broadcast_to(kv, (tq, n_dp // sharers, sharers, kv_need)).reshape(tq, n_dp, kv_need)
    second = jnp.transpose(jnp.concatenate([query, kv], axis=2), (1, 0, 2))
    second = lax.all_to_all(second, "dp", 0, 0)
    second = spread_owner(second, n_owner)

    total = scatter_sum(
        lambda groups: pair_product(groups, first, projection), n_dp, z, x, outer, inner
    )
    total = total.reshape(n_owner, tq, rows_own)
    grad_input = jnp.take(total, jnp.arange(n_owner) ^ owner, axis=0).reshape(group, rows_own)

    split = sharers > 1 and row_blocks % sharers == 0
    kv_rows = row_blocks // sharers if split else row_blocks
    member = dp % sharers
    base = member * kv_rows if split else member * 0
    kv_update = block_updates(
        jnp.stack([owner, base]), inputs, second, q_own // BLOCK, kv_rows, kv_need // BLOCK
    )
    parts = kv_update.reshape(kv_update.shape[0], -1, kv_own)

    def part_of(m):
        return lax.dynamic_index_in_dim(parts, m, 1, keepdims=False)

    if split:
        update_kv = jnp.zeros((sharers, kv_update.shape[0], kv_own), jnp.bfloat16)
        for s in range(sharers):
            pairs = [(i, i // sharers * sharers + (i + s) % sharers) for i in range(n_dp)]
            piece = part_of((member + s) % sharers)
            if s:
                piece = lax.ppermute(piece, "dp", pairs)
            update_kv = lax.dynamic_update_index_in_dim(
                update_kv, piece, (member - s) % sharers, 0
            )
        update_kv = update_kv.reshape(rows_own, kv_own)
    elif sharers > 1:
        update_kv = part_of(member)
    else:
        update_kv = kv_update
    update_query = block_updates(
        jnp.stack([owner, owner * 0]), inputs, second, 0, row_blocks, q_own // BLOCK
    )
    return (grad_input, update_query, update_kv)


def solution(mesh):
    placed = (P("dp", "owner"), P("dp", "owner"), P("owner", "dp"))
    return jax.shard_map(
        body,
        mesh=mesh,
        in_specs=placed,
        out_specs=(P("dp", "owner"), P("owner", "dp"), P("owner", "dp")),
        check_vma=False,
    )
```

```python
import functools
import math

import jax
import jax.numpy as jnp
import numpy as np
from jax import lax
from jax.experimental import pallas as pl
from jax.experimental.pallas import tpu as pltpu
from jax.sharding import PartitionSpec as P


BLOCK = 512
QW = 8192


def inner_size(n):
    return 1 << (int(math.log2(n)) // 2)


def swap_owner(x, mask, n_owner):
    return lax.ppermute(x, "owner", [(i, i ^ mask) for i in range(n_owner)])


def spread_far(x, n_owner):
    bit = n_owner // 2
    return {0: x, bit: swap_owner(x, bit, n_owner)} if bit else {0: x}


def spread_near(pieces, n_owner):
    pieces = dict(pieces)
    bit = n_owner // 4
    while bit:
        pieces.update({k | bit: swap_owner(p, bit, n_owner) for k, p in pieces.items()})
        bit //= 2
    return [pieces[k] for k in range(n_owner)]


def pair_kernel(tab, *refs, n_owner, pair):
    xs, w_ref, o_ref = refs[: pair * n_owner], refs[-2], refs[-1]
    rows = jnp.concatenate([r[0] for r in xs], axis=0)
    out = lax.dot_general(
        rows, w_ref[...], (((1,), (1,)), ((), ())), preferred_element_type=jnp.float32
    )
    o_ref[...] = out.astype(o_ref.dtype).reshape(o_ref.shape)


def pair_product(tab, pieces, w, tile=512):
    n_owner, pair = len(pieces), tab.shape[0]
    _, tq, cols = pieces[0].shape
    feats = w.shape[0]
    tile = min(tile, feats)
    xspec = [
        pl.BlockSpec((1, tq, cols), lambda j, t, i=i: (t[i], 0, 0))
        for i in range(pair)
        for _ in range(n_owner)
    ]
    return pl.pallas_call(
        functools.partial(pair_kernel, n_owner=n_owner, pair=pair),
        grid_spec=pltpu.PrefetchScalarGridSpec(
            num_scalar_prefetch=1,
            grid=(feats // tile,),
            in_specs=xspec + [pl.BlockSpec((tile, cols), lambda j, t: (j, 0))],
            out_specs=pl.BlockSpec((pair, n_owner * tq, tile), lambda j, t: (0, 0, j)),
        ),
        out_shape=jax.ShapeDtypeStruct((pair, n_owner * tq, feats), jnp.bfloat16),
        compiler_params=pltpu.CompilerParams(vmem_limit_bytes=40 << 20),
        cost_estimate=pl.CostEstimate(
            flops=2 * pair * n_owner * tq * cols * feats,
            bytes_accessed=2 * (feats * cols + pair * n_owner * tq * (cols + feats)),
            transcendentals=0,
        ),
        name="pair_product",
    )(tab, *(pieces * pair), w)


def update_kernel(tab, l_ref, *refs, n_owner):
    xs, o_ref = refs[:n_owner], refs[-1]
    width = o_ref.shape[-1]
    acc = None
    for k in range(n_owner):
        left = l_ref[:, tab[0] ^ k]
        left = left.reshape(-1, width)
        right = xs[k][...].reshape(-1, width)
        term = lax.dot_general(
            left, right, (((0,), (0,)), ((), ())), preferred_element_type=jnp.float32
        )
        acc = term if acc is None else acc + term
    g = acc.astype(jnp.bfloat16)
    stat = lax.dot_general(
        g, g, (((1,), (1,)), ((), ())), preferred_element_type=jnp.float32
    )
    mean = jnp.sum(stat * stat) * (1.0 / (width * width))
    scale = math.sqrt(width) * jnp.sqrt(jnp.full((1, 1), mean + 1e-06))
    normed = (stat * (1.0 / scale)).astype(jnp.bfloat16)
    once = 5.0 * g.astype(jnp.float32) - jnp.dot(
        normed, g, preferred_element_type=jnp.float32
    )
    twice = 5.0 * once - jnp.dot(
        normed, once.astype(jnp.bfloat16), preferred_element_type=jnp.float32
    )
    factor = (math.sqrt(width) / 16.0) * lax.rsqrt(scale)
    o_ref[...] = (twice * factor).astype(o_ref.dtype)


def block_updates(tab, inputs, pieces, first_col, n_rows, n_cols, into=None, first_row=0, rows=None):
    count, n_owner, tq, _ = inputs.shape
    width = BLOCK
    tokens = count * n_owner * tq
    rows = n_rows if rows is None else rows
    extra = [] if into is None else [into]
    return pl.pallas_call(
        functools.partial(update_kernel, n_owner=n_owner),
        grid_spec=pltpu.PrefetchScalarGridSpec(
            num_scalar_prefetch=1,
            grid=(n_rows, n_cols),
            in_specs=[
                pl.BlockSpec((count, n_owner, tq, width), lambda r, c, t: (0, 0, 0, r + t[1]))
            ]
            + [
                pl.BlockSpec((count, tq, width), lambda r, c, t: (0, 0, c + first_col))
                for _ in range(n_owner)
            ]
            + [pl.BlockSpec(memory_space=pl.ANY) for _ in extra],
            out_specs=pl.BlockSpec((width, width), lambda r, c, t: (r + first_row, c)),
        ),
        out_shape=jax.ShapeDtypeStruct((rows * width, n_cols * width), jnp.bfloat16),
        input_output_aliases={2 + n_owner: 0} if extra else {},
        compiler_params=pltpu.CompilerParams(vmem_limit_bytes=56 << 20),
        cost_estimate=pl.CostEstimate(
            flops=n_rows * n_cols * (2 * tokens * width * width + 6 * width**3),
            bytes_accessed=2 * n_rows * n_cols * tokens * width * 2,
            transcendentals=0,
        ),
        name="block_updates",
    )(tab, inputs, *pieces, *extra)


def scatter_sum(products, z, x, outer, inner):
    order = np.zeros((outer, outer), np.int32)
    for i in range(outer):
        order[i] = sorted(range(outer), key=lambda t: (-abs(t - i), t != i and t < i))
    slot = np.argsort(order, axis=1)
    order_c = jnp.asarray(order)
    groups = jnp.stack(
        [order_c[z, k] * inner + (x + s) % inner for k in range(outer) for s in range(inner)]
    )
    first = products(groups[:inner])
    rest = products(groups[inner:])
    sums = []
    for k in range(outer):
        part = first if k == 0 else rest[(k - 1) * inner : k * inner]
        total = part[0].astype(jnp.float32)
        for s in range(1, inner):
            pairs = [
                (a * inner + b, a * inner + (b + s) % inner)
                for a in range(outer)
                for b in range(inner)
            ]
            other = lax.ppermute(part[s], "dp", pairs)
            total = total + other.astype(jnp.float32)
        sums.append(total.astype(jnp.bfloat16))

    def chosen(step, sign):
        table = np.zeros(outer, np.int32)
        pairs = []
        for i in range(outer):
            target = i + sign * (outer - step)
            if 0 <= target < outer:
                table[i] = slot[i, target]
                pairs += [
                    (i * inner + b, (i + sign) * inner + b) for b in range(inner)
                ]
        used = sorted(set(table[[p[0] // inner for p in pairs]].tolist()))
        value = sums[used[0]]
        for u in used[1:]:
            value = jnp.where(jnp.asarray(table)[z] == u, sums[u], value)
        return value, pairs

    running = {1: None, -1: None}
    for step in range(1, outer):
        for sign in (1, -1):
            value, pairs = chosen(step, sign)
            if running[sign] is not None:
                value = (value.astype(jnp.float32) + running[sign].astype(jnp.float32)).astype(
                    jnp.bfloat16
                )
            running[sign] = lax.ppermute(value, "dp", pairs)
    own = sums[outer - 1].astype(jnp.float32)
    if outer > 1:
        own = own + running[1].astype(jnp.float32) + running[-1].astype(jnp.float32)
    return own.astype(jnp.bfloat16)


def body(layer_input, output_grads, projection):
    n_dp, n_owner = lax.axis_size("dp"), lax.axis_size("owner")
    dp, owner = lax.axis_index("dp"), lax.axis_index("owner")
    inner = inner_size(n_dp)
    outer = n_dp // inner
    z, x = dp // inner, dp % inner
    group, rows_own = layer_input.shape
    cols_own = projection.shape[1]
    all_cols = cols_own * n_dp
    tq = group // n_owner
    q_own = QW // n_dp
    kv_own = (all_cols - QW) // n_dp
    sharers = max(1, BLOCK // kv_own)
    kv_need = max(kv_own, BLOCK)
    row_blocks = rows_own // BLOCK
    halves = 2 if row_blocks % (2 * sharers) == 0 else 1
    half_rows = row_blocks // halves

    inputs = []
    for h in range(halves):
        part = layer_input[:, h * half_rows * BLOCK : (h + 1) * half_rows * BLOCK]
        part = lax.all_gather(part, "dp", axis=0, tiled=True)
        inputs.append(part.reshape(n_dp, n_owner, tq, half_rows * BLOCK))

    spread = lax.all_to_all(output_grads.reshape(n_owner, tq, output_grads.shape[1]), "owner", 0, 0)
    flat = jnp.transpose(spread, (1, 0, 2)).reshape(tq, all_cols)
    first = jnp.transpose(flat.reshape(tq, n_dp, cols_own), (1, 0, 2))
    first = lax.all_to_all(first, "dp", 0, 0)
    first = spread_far(first, n_owner)
    query = flat[:, :QW].reshape(tq, n_dp, q_own)
    kv = flat[:, QW:].reshape(tq, n_dp // sharers, 1, kv_need)
    kv = jnp.broadcast_to(kv, (tq, n_dp // sharers, sharers, kv_need)).reshape(tq, n_dp, kv_need)
    second = jnp.transpose(jnp.concatenate([query, kv], axis=2), (1, 0, 2))
    second = lax.all_to_all(second, "dp", 0, 0)
    first, second = lax.optimization_barrier((first, second))
    first = spread_near(first, n_owner)
    second = spread_far(second, n_owner)
    second = spread_near(second, n_owner)

    total = scatter_sum(lambda groups: pair_product(groups, first, projection), z, x, outer, inner)
    total = total.reshape(n_owner, tq, rows_own)
    grad_input = jnp.concatenate(
        [lax.dynamic_index_in_dim(total, owner ^ k, 0, keepdims=False) for k in range(n_owner)], axis=0
    )

    split = sharers > 1 and half_rows % sharers == 0
    kv_rows = half_rows // sharers if split else half_rows
    member = dp % sharers
    base = member * kv_rows if split else member * 0
    kv_tab, q_tab = jnp.stack([owner, base]), jnp.stack([owner, owner * 0])
    kv_parts, update_query = [], None
    for h in range(halves):
        kv_parts.append(
            block_updates(kv_tab, inputs[h], second, q_own // BLOCK, kv_rows, kv_need // BLOCK)
        )
        update_query = block_updates(
            q_tab, inputs[h], second, 0, half_rows, q_own // BLOCK,
            update_query, h * half_rows, row_blocks,
        )
    kv_update = jnp.stack(kv_parts)
    parts = kv_update.reshape(halves, kv_update.shape[1], -1, kv_own)

    def part_of(m):
        return lax.dynamic_index_in_dim(parts, m, 2, keepdims=False)

    if split:
        update_kv = jnp.zeros((halves, sharers, kv_update.shape[1], kv_own), jnp.bfloat16)
        for s in range(sharers):
            pairs = [(i, i // sharers * sharers + (i + s) % sharers) for i in range(n_dp)]
            piece = part_of((member + s) % sharers)
            if s:
                piece = lax.ppermute(piece, "dp", pairs)
            update_kv = lax.dynamic_update_index_in_dim(
                update_kv, piece, (member - s) % sharers, 1
            )
        update_kv = update_kv.reshape(rows_own, kv_own)
    elif sharers > 1:
        update_kv = part_of(member).reshape(rows_own, kv_own)
    else:
        update_kv = kv_update.reshape(rows_own, kv_own)
    return (grad_input, update_query, update_kv)


def solution(mesh):
    placed = (P("dp", "owner"), P("dp", "owner"), P("owner", "dp"))
    return jax.shard_map(
        body,
        mesh=mesh,
        in_specs=placed,
        out_specs=(P("dp", "owner"), P("owner", "dp"), P("owner", "dp")),
        check_vma=False,
    )
```
